256 devices in a mesh: sec: 2 (over x_hi), col: 8 (over y, x_lo), elem: 16 (over z, core).
Axes of the slice: x: 4 (x_hi: 2, x_lo: 2; x = x_hi * 2 + x_lo), y: 4, z: 8, core: 2. Of those that a mesh axis runs over, the one named last changes fastest.
Arguments:
- probes: float32 [256, 96, 256], P('col', 'elem'), may hold values from -6 to 6
- jacobian: float32 [2, 96, 7, 256, 256], P('sec', 'elem'), may hold values from -0.0625 to 0.0625
- neighbors: int32 [96, 7], P('elem'), may hold values from 0 to 95, as said below
- stations: int32 [1024], P('elem'), may hold values from 0 to 95, as said below
- obs_weights: float32 [1024, 256], P('elem'), may hold values from -0.75 to 0.75
Outputs:
- hess_probes: float32 [256, 96, 256], P('col', 'elem', 'sec')
- gram: float32 [256, 256], P('col')
The draws below stay inside these ranges and needn't reach their ends.
Inputs may be any that keep to these rules, and one draw needn't show every extreme that they name: `neighbors`: row e lists the 7 elements e - 3 to e + 3, taken modulo 96, each once, in an order drawn for each row. Station i lies in one of the 6 elements from (i // 64) * 6 on; every element holds one or more stations.
All inputs are finite; a program needn't handle non-finite values.
Results may differ from the reference program's by a relative error of at most 0.0001.
Values sent between devices are 32-bit elements; how exact they have to be, the bound alone decides.
No kernel may reach another device: no remote copies, remote signals or barrier semaphores. Data moves between devices by JAX's collectives and lax.ppermute only.
A program may use at most 64 MiB of HBM per device.

```python
from functools import partial
import jax
import jax.numpy as jnp
from jax import lax

ORDER = 256
NBRS = 7
EL_DEV = 6
STAT_DEV = 64
STEPS = 2
SECS = 2
ELEMS = 96
COLS = 256
STATIONS = 1024


def draw_neighbors(key, part):
    element_ids = jnp.arange(ELEMS, dtype=jnp.int32)
    row_keys = jax.random.split(jax.random.fold_in(key, 11), ELEMS)
    shuffle = partial(jax.random.permutation, x=NBRS)
    orders = jax.vmap(shuffle)(row_keys).astype(jnp.int32)
    radius = (NBRS - 1) // 2
    return ((element_ids[:, None] + orders - radius) % ELEMS).astype(jnp.int32)


def draw_stations(key, part):
    positions = jnp.arange(STATIONS, dtype=jnp.int32)
    block_ids = positions // STAT_DEV
    in_block = positions % STAT_DEV
    key_first, key_second = jax.random.split(jax.random.fold_in(key, 23))
    offsets = jax.random.randint(key_first, (STATIONS // STAT_DEV,), 0, EL_DEV).astype(jnp.int32)
    extras = jax.random.randint(key_second, (STATIONS,), 0, EL_DEV).astype(jnp.int32)
    within = jnp.where(in_block < EL_DEV, (in_block + offsets[block_ids]) % EL_DEV, extras)
    return (block_ids * EL_DEV + within).astype(jnp.int32)


def levels(own_key, shape, cuts, smallest, top_value):
    loudness = 1.0
    for dim, blocks in cuts:
        draws = jax.random.uniform(jax.random.fold_in(jax.random.fold_in(own_key, 6), dim), (blocks,), jnp.float32, smallest / len(cuts), top_value / len(cuts))
        loudness = loudness * jnp.repeat(jnp.exp(draws), shape[dim] // blocks).reshape((-1,) + (1,) * (len(shape) - 1 - dim))
    return loudness


def gaussian(own_key, dims, scale, reach, pieces=(), held_as=jnp.bfloat16):
    entries = scale * jax.random.normal(own_key, dims, jnp.float32)
    if pieces:
        entries = entries * levels(own_key, dims, pieces, -0.22, 0.18)
    return jnp.clip(entries, -reach, reach).astype(held_as)


def setup_inputs(seed: int = 0) -> dict:
    key_list = jax.random.split(jax.random.key(seed), 6)
    probes = gaussian(key_list[0], (COLS, ELEMS, ORDER), 1.0, 6.0, ((0, 8), (1, 16)), jnp.float32)
    jacobian = gaussian(key_list[1], (SECS, ELEMS, NBRS, ORDER, ORDER), (4 * NBRS * ORDER) ** -0.5, 0.0625, ((0, 2), (1, 16)), jnp.float32)
    neighbors = draw_neighbors(jax.random.fold_in(key_list[5], 71), 0)
    stations = draw_stations(jax.random.fold_in(key_list[5], 71), 0)
    obs_weights = gaussian(key_list[4], (STATIONS, ORDER), (ORDER // 4) ** -0.5, 0.75, ((0, 16),), jnp.float32)
    return {"probes": probes, "jacobian": jacobian, "neighbors": neighbors, "stations": stations, "obs_weights": obs_weights}


PRECISE = lax.Precision.HIGHEST


def tangent(vector, blocks, neighbors):
    gathered = jnp.take(vector, neighbors, axis=1)
    return vector + jnp.einsum("cekI,ekJI->ceJ", gathered, blocks, precision=PRECISE)


def adjoint_step(vector, blocks, neighbors):
    products = jnp.einsum("ceJ,ekJI->cekI", vector, blocks, precision=PRECISE)
    flattened = products.reshape(products.shape[0], -1, products.shape[-1])
    returned = jnp.zeros_like(vector).at[:, neighbors.reshape(-1)].add(flattened)
    return vector + returned


def observe(vector, stations, obs_weights):
    sampled = jnp.take(vector, stations, axis=1)
    readings = jnp.einsum("csI,sI->cs", sampled, obs_weights, precision=PRECISE)
    weighted = readings[:, :, None] * obs_weights[None, :, :]
    return jnp.zeros_like(vector).at[:, stations].add(weighted)


def reference(probes, jacobian, neighbors, stations, obs_weights):
    states = []
    current = probes
    for section in range(SECS):
        for repeat in range(STEPS):
            current = tangent(current, jacobian[section], neighbors)
        states.append(current)
    adjoint = observe(states[-1], stations, obs_weights)
    for section in range(SECS - 1, -1, -1):
        for repeat in range(STEPS):
            adjoint = adjoint_step(adjoint, jacobian[section], neighbors)
        if section > 0:
            adjoint = adjoint + observe(states[section - 1], stations, obs_weights)
    flat_probes = probes.reshape(COLS, -1)
    flat_hess = adjoint.reshape(COLS, -1)
    gram = jnp.einsum("ax,bx->ab", flat_probes, flat_hess, precision=PRECISE) / (ELEMS * ORDER)
    return adjoint, gram
```

```python
import functools

import jax
import jax.numpy as jnp
from jax import lax
from jax.experimental import pallas as pl
from jax.experimental.pallas import tpu as pltpu
from jax.sharding import PartitionSpec as P

NBRS = 7
RADIUS = 3
STEPS = 2
PRECISE = lax.Precision.HIGHEST
BF16 = jnp.bfloat16
F32 = jnp.float32
NN = (((1,), (0,)), ((), ()))
NT = (((1,), (1,)), ((), ()))

IN_VMEM = pl.BlockSpec(memory_space=pltpu.VMEM)
IN_SMEM = pl.BlockSpec(memory_space=pltpu.SMEM)
IN_HBM = pl.BlockSpec(memory_space=pltpu.HBM)


def call(body, name, outs, in_specs, scratch=(), vmem=4 << 20, flops=10**8, moved=10**6):
    single = not isinstance(outs, tuple)
    return pl.pallas_call(
        body,
        name=name,
        out_shape=outs,
        in_specs=in_specs,
        out_specs=IN_VMEM if single else (IN_VMEM,) * len(outs),
        scratch_shapes=list(scratch),
        compiler_params=pltpu.CompilerParams(vmem_limit_bytes=vmem),
        cost_estimate=pl.CostEstimate(flops=flops, bytes_accessed=moved, transcendentals=0),
    )


def vmem(shape, dtype=F32):
    return pltpu.VMEM(shape, dtype)


def split(value):
    high = value.astype(BF16)
    low = (value - high.astype(F32)).astype(BF16)
    return high, low


def store_split(pair_ref, slot, value):
    rows = value.shape[0]
    high, low = split(value)
    pair_ref[slot, :rows] = high
    pair_ref[slot, rows:] = low


def product(pair_ref, slot, high_ref, low_ref, block, dims):
    rows = pair_ref.shape[1] // 2
    both = lax.dot_general(pair_ref[slot], high_ref[block], dims, preferred_element_type=F32)
    rest = lax.dot_general(
        pair_ref[slot, :rows], low_ref[block], dims, preferred_element_type=F32
    )
    return both[:rows] + both[rows:] + rest


def odd_device():
    return lax.rem(lax.axis_index("elem"), 2) == 1


def prepare_body(elem_total, nbr_ref, jac_ref, high_ref, low_ref, buffer, sems):
    elems = buffer.shape[0]
    copies = [
        pltpu.make_async_copy(jac_ref.at[0, e], buffer.at[e], sems.at[e]) for e in range(elems)
    ]
    for copy in copies:
        copy.start()
    first = lax.axis_index("elem") * elems
    odd = odd_device()
    for e in range(elems):
        copies[e].wait()

        def one(k, carry, e=e):
            offset = lax.rem(nbr_ref[e, k] - (first + e) + RADIUS + elem_total, elem_total)
            slot = e * NBRS + offset
            slot = jnp.where(odd, elems * NBRS - 1 - slot, slot)
            high, low = split(buffer[e, k])
            high_ref[slot] = high
            low_ref[slot] = low
            return carry

        lax.fori_loop(0, NBRS, one, 0)


def mirror_body(field_ref, out_ref):
    elems = field_ref.shape[0]
    odd = odd_device()
    for u in range(elems):
        out_ref[u] = field_ref[jnp.where(odd, elems - 1 - u, u)]


def tangent_local_body(field_ref, high_ref, low_ref, total_ref, pair_ref):
    elems = field_ref.shape[0]
    for e in range(elems):
        store_split(pair_ref, e, field_ref[e])
    for e in range(elems):
        total = field_ref[e]
        for m in range(max(0, e - RADIUS), min(elems, e + RADIUS + 1)):
            total += product(pair_ref, m, high_ref, low_ref, e * NBRS + m - e + RADIUS, NT)
        total_ref[e] = total


def tangent_edge_body(total_ref, outer_ref, inner_ref, high_ref, low_ref, field_ref, pair_ref):
    elems = total_ref.shape[0]
    for i in range(RADIUS):
        store_split(pair_ref, i, outer_ref[i])
        store_split(pair_ref, RADIUS + i, inner_ref[i])
    for e in range(elems):
        total = total_ref[e]
        for m in range(e - RADIUS, e + RADIUS + 1):
            if m < 0:
                slot = -1 - m
            elif m >= elems:
                slot = RADIUS + (elems + RADIUS - 1 - m)
            else:
                continue
            total += product(pair_ref, slot, high_ref, low_ref, e * NBRS + m - e + RADIUS, NT)
        field_ref[e] = total


def edge_products(pair_ref, high_ref, low_ref, outer_ref, inner_ref, elems):
    for i in range(RADIUS):
        for ref, m in ((outer_ref, -1 - i), (inner_ref, elems + RADIUS - 1 - i)):
            total = None
            for e in range(max(0, m - RADIUS), min(elems, m + RADIUS + 1)):
                term = product(pair_ref, e, high_ref, low_ref, e * NBRS + m - e + RADIUS, NN)
                total = term if total is None else total + term
            ref[i] = total


def observe_body(
    state0_ref, state1_ref, stations_ref, weights_ref, high_ref, low_ref,
    seen_ref, readings_ref, outer_ref, inner_ref, pair_ref, state_ref,
):
    elems, cols, dofs = state0_ref.shape
    count = weights_ref.shape[0]
    section = lax.axis_index("sec")

    @pl.when(section == 0)
    def _():
        state_ref[...] = state0_ref[...]

    @pl.when(section != 0)
    def _():
        state_ref[...] = state1_ref[...]

    flat = state_ref[...].reshape(elems * cols, dofs)
    weights = weights_ref[...]
    raw = lax.dot_general(flat, weights, NT, precision=PRECISE, preferred_element_type=F32)
    local = stations_ref[...] - lax.axis_index("elem") * elems
    odd = odd_device()
    readings = jnp.zeros((cols, count), F32)
    for u in range(elems):
        here = local == jnp.where(odd, elems - 1 - u, u)
        part = jnp.where(here, raw[u * cols : (u + 1) * cols], 0.0)
        readings += part
        seen = lax.dot_general(part, weights, NN, precision=PRECISE, preferred_element_type=F32)
        seen_ref[u] = seen
        store_split(pair_ref, u, seen)
    readings_ref[...] = readings
    edge_products(pair_ref, high_ref, low_ref, outer_ref, inner_ref, elems)


def adjoint_local_body(field_ref, high_ref, low_ref, total_ref, pair_ref):
    elems = field_ref.shape[0]
    for e in range(elems):
        store_split(pair_ref, e, field_ref[e])
    for m in range(elems):
        total = field_ref[m]
        for e in range(max(0, m - RADIUS), min(elems, m + RADIUS + 1)):
            total += product(pair_ref, e, high_ref, low_ref, e * NBRS + m - e + RADIUS, NN)
        total_ref[m] = total


def adjoint_edge_body(
    total_ref, outer_in_ref, inner_in_ref, high_ref, low_ref,
    field_ref, outer_ref, inner_ref, pair_ref,
):
    elems = total_ref.shape[0]
    for i in range(RADIUS):
        for u, ref in ((i, outer_in_ref), (RADIUS + i, inner_in_ref)):
            value = total_ref[u] + ref[i]
            field_ref[u] = value
            store_split(pair_ref, u, value)
    edge_products(pair_ref, high_ref, low_ref, outer_ref, inner_ref, elems)


def adjoint_join_body(total_ref, outer_in_ref, inner_in_ref, field_ref):
    for i in range(RADIUS):
        field_ref[i] = total_ref[i] + outer_in_ref[i]
        field_ref[RADIUS + i] = total_ref[RADIUS + i] + inner_in_ref[i]


def add_edge_body(
    seen_ref, back_ref, high_ref, low_ref, field_ref, outer_ref, inner_ref, pair_ref
):
    elems = seen_ref.shape[0]
    for u in range(elems):
        value = seen_ref[u] + back_ref[u]
        field_ref[u] = value
        store_split(pair_ref, u, value)
    edge_products(pair_ref, high_ref, low_ref, outer_ref, inner_ref, elems)


def finish_body(total_ref, outer_in_ref, inner_in_ref, lower_ref, upper_ref):
    elems, cols, dofs = total_ref.shape
    half = dofs // 2
    odd = odd_device()
    for u in range(elems):
        ref = outer_in_ref if u < RADIUS else inner_in_ref
        value = total_ref[u] + ref[u % RADIUS]
        place = jnp.where(odd, elems - 1 - u, u)
        lower_ref[place] = value[:, :half]
        upper_ref[place] = value[:, half:]


def gram_body(stack_ref, out_ref):
    own = lax.axis_index("col")
    cols = stack_ref.shape[1]
    mine = stack_ref[0]
    blocks = [stack_ref[jnp.bitwise_xor(own, j)] for j in range(stack_ref.shape[0])]
    every = jnp.concatenate(blocks, axis=0)
    out_ref[...] = lax.dot_general(
        mine, every, NT, precision=PRECISE, preferred_element_type=F32
    )


def swap(value, axis, distance):
    count = lax.axis_size(axis)
    return lax.ppermute(value, axis, [(i, i ^ distance) for i in range(count)])


def exchange(outer, inner):
    count = lax.axis_size("elem")
    on_chip = [(i, i ^ 1) for i in range(count)]
    off_chip = [(i, (i + (1 if i % 2 else -1)) % count) for i in range(count)]
    inner_in = lax.ppermute(inner, "elem", on_chip)
    outer_in = lax.ppermute(outer, "elem", off_chip)
    return outer_in, inner_in


def per_device(probes, jacobian, neighbors, stations, obs_weights):
    cols, elems, dofs = probes.shape
    elem_total = elems * lax.axis_size("elem")
    blocks = elems * NBRS
    field = vmem((elems, cols, dofs))
    edge = vmem((RADIUS, cols, dofs))
    half = vmem((elems, cols, dofs // 2))
    pair = pltpu.VMEM((elems, 2 * cols, dofs), BF16)
    count = obs_weights.shape[0]

    prepare = call(
        functools.partial(prepare_body, elem_total), "prepare",
        (vmem((blocks, dofs, dofs), BF16),) * 2, [IN_SMEM, IN_HBM],
        (pltpu.VMEM((elems, NBRS, dofs, dofs), F32), pltpu.SemaphoreType.DMA((elems,))),
        vmem=16 << 20, moved=2 * 10**7,
    )
    mirror = call(mirror_body, "mirror", field, [IN_VMEM])
    tangent_local = call(
        tangent_local_body, "tangent_local", field, [IN_VMEM] * 3, (pair,), flops=2 * 10**9
    )
    tangent_edge = call(
        tangent_edge_body, "tangent_edge", field, [IN_VMEM] * 5, (pair,), flops=10**9
    )
    observe = call(
        observe_body, "observe", (field, vmem((cols, count)), edge, edge), [IN_VMEM] * 6,
        (pair, pltpu.VMEM((elems, cols, dofs), F32)), flops=10**9,
    )
    adjoint_local = call(
        adjoint_local_body, "adjoint_local", field, [IN_VMEM] * 3, (pair,), flops=2 * 10**9
    )
    adjoint_edge = call(
        adjoint_edge_body, "adjoint_edge", (field, edge, edge), [IN_VMEM] * 5, (pair,),
        flops=10**9,
    )
    adjoint_join = call(adjoint_join_body, "adjoint_join", field, [IN_VMEM] * 3)
    add_edge = call(
        add_edge_body, "add_edge", (field, edge, edge), [IN_VMEM] * 4, (pair,), flops=10**9
    )
    finish = call(finish_body, "finish", (half, half), [IN_VMEM] * 3)
    col_count = lax.axis_size("col")
    gram_part = call(gram_body, "gram_part", vmem((cols, cols * col_count)), [IN_VMEM])

    def tangent(value, high, low):
        for _ in range(STEPS):
            outer_in, inner_in = exchange(value[:RADIUS], value[RADIUS:])
            total = tangent_local(value, high, low)
            value = tangent_edge(total, outer_in, inner_in, high, low)
        return value

    def adjoint(value, outer, inner, high, low):
        for step in range(STEPS):
            outer_in, inner_in = exchange(outer, inner)
            total = adjoint_local(value, high, low)
            if step + 1 < STEPS:
                value, outer, inner = adjoint_edge(total, outer_in, inner_in, high, low)
        return total, outer_in, inner_in

    section = lax.axis_index("sec")
    high, low = prepare(neighbors, jacobian)
    start = mirror(jnp.transpose(probes, (1, 0, 2)))
    state0 = tangent(start, high, low)
    incoming = lax.ppermute(state0, "sec", [(0, 1)])
    state1 = tangent(incoming, high, low)
    seen, readings, outer, inner = observe(
        state0, state1, stations.reshape(1, count), obs_weights, high, low
    )
    joined = adjoint_join(*adjoint(seen, outer, inner, high, low))
    back = lax.ppermute(joined, "sec", [(1, 0)])
    value, outer, inner = add_edge(seen, back, high, low)
    lower, upper = finish(*adjoint(value, outer, inner, high, low))
    upper = lax.ppermute(upper, "sec", [(0, 1)])
    hess = jnp.transpose(jnp.where(section == 0, lower, upper), (1, 0, 2))

    stack = readings[None]
    distance = 1
    while distance < col_count:
        stack = jnp.concatenate([stack, swap(stack, "col", distance)], axis=0)
        distance *= 2
    gram = gram_part(stack)
    distance = 1
    while distance < lax.axis_size("elem"):
        gram = gram + swap(gram, "elem", distance)
        distance *= 2
    gram = gram + swap(gram, "sec", 1)
    return hess, gram * (1.0 / (elem_total * dofs))


def solution(mesh):
    in_specs = (
        P("col", "elem", None),
        P("sec", "elem", None, None, None),
        P("elem", None),
        P("elem"),
        P("elem", None),
    )
    out_specs = (P("col", "elem", "sec"), P("col", None))
    return jax.shard_map(
        per_device, mesh=mesh, in_specs=in_specs, out_specs=out_specs, check_vma=False
    )
```

```python
import functools

import jax
import jax.numpy as jnp
from jax import lax
from jax.experimental import pallas as pl
from jax.experimental.pallas import tpu as pltpu
from jax.sharding import PartitionSpec as P

NBRS = 7
RADIUS = 3
STEPS = 2
WORK = {
    "prepare": 30,
    "mirror": 30,
    "tangent_near": 30,
    "tangent_far": 30,
    "observe": 200,
    "adjoint_local": 100,
    "adjoint_outer": 400,
    "adjoint_inner": 100,
    "seen_outer": 100,
    "finish": 1000,
    "gram_part": 30,
}
PRECISE = lax.Precision.HIGHEST
BF16 = jnp.bfloat16
F32 = jnp.float32
NN = (((1,), (0,)), ((), ()))
NT = (((1,), (1,)), ((), ()))

IN_VMEM = pl.BlockSpec(memory_space=pltpu.VMEM)
IN_SMEM = pl.BlockSpec(memory_space=pltpu.SMEM)
IN_HBM = pl.BlockSpec(memory_space=pltpu.HBM)


def call(body, name, outs, in_specs, scratch=(), vmem=4 << 20, moved=10**5):
    single = not isinstance(outs, tuple)
    return pl.pallas_call(
        body,
        name=name,
        out_shape=outs,
        in_specs=in_specs,
        out_specs=IN_VMEM if single else (IN_VMEM,) * len(outs),
        scratch_shapes=list(scratch),
        compiler_params=pltpu.CompilerParams(vmem_limit_bytes=vmem),
        cost_estimate=pl.CostEstimate(flops=WORK[name] * 10**7, bytes_accessed=moved, transcendentals=0),
    )


def vmem(shape, dtype=F32):
    return pltpu.VMEM(shape, dtype)


def split(value):
    high = value.astype(BF16)
    low = (value - high.astype(F32)).astype(BF16)
    return high, low


def store_split(pair_ref, slot, value):
    rows = value.shape[0]
    high, low = split(value)
    pair_ref[slot, :rows] = high
    pair_ref[slot, rows:] = low


def product(pair_ref, slot, high_ref, low_ref, block, dims):
    rows = pair_ref.shape[1] // 2
    both = lax.dot_general(pair_ref[slot], high_ref[block], dims, preferred_element_type=F32)
    rest = lax.dot_general(
        pair_ref[slot, :rows], low_ref[block], dims, preferred_element_type=F32
    )
    return both[:rows] + both[rows:] + rest


def odd_device():
    return lax.rem(lax.axis_index("elem"), 2) == 1


def prepare_body(elem_total, nbr_ref, jac_ref, high_ref, low_ref, buffer, sems):
    elems = buffer.shape[0]
    copies = [
        [
            pltpu.make_async_copy(jac_ref.at[0, e, k], buffer.at[e, k], sems.at[e, k])
            for k in range(NBRS)
        ]
        for e in range(elems)
    ]
    for row in copies:
        for copy in row:
            copy.start()
    first = lax.axis_index("elem") * elems
    odd = odd_device()
    for e in range(elems):
        for k in range(NBRS):
            copies[e][k].wait()
            offset = lax.rem(nbr_ref[e, k] - (first + e) + RADIUS + elem_total, elem_total)
            slot = e * NBRS + offset
            slot = jnp.where(odd, elems * NBRS - 1 - slot, slot)
            high, low = split(buffer[e, k])
            high_ref[slot] = high
            low_ref[slot] = low


def mirror_body(field_ref, outer_ref, inner_ref):
    elems = field_ref.shape[0]
    odd = odd_device()
    for i in range(RADIUS):
        outer_ref[i] = field_ref[jnp.where(odd, elems - 1 - i, i)]
        inner_ref[i] = field_ref[jnp.where(odd, elems - 1 - RADIUS - i, RADIUS + i)]


def block(e, m):
    return e * NBRS + m - e + RADIUS


def tangent_near_body(
    outer_ref, inner_ref, halo_ref, high_ref, low_ref, outer_out, inner_out, pair_ref
):
    elems = 2 * RADIUS
    for i in range(RADIUS):
        store_split(pair_ref, i, outer_ref[i])
        store_split(pair_ref, RADIUS + i, inner_ref[i])
        store_split(pair_ref, elems + RADIUS - 1 - i, halo_ref[i])
    for e in range(elems):
        total = outer_ref[e] if e < RADIUS else inner_ref[e - RADIUS]
        for m in range(max(0, e - RADIUS), e + RADIUS + 1):
            total += product(pair_ref, m, high_ref, low_ref, block(e, m), NT)
        if e < RADIUS:
            outer_out[e] = total
        else:
            inner_out[e - RADIUS] = total


def tangent_far_body(outer_ref, halo_ref, high_ref, low_ref, outer_out, pair_ref):
    for i in range(RADIUS):
        store_split(pair_ref, i, halo_ref[i])
    for e in range(RADIUS):
        total = outer_ref[e]
        for i in range(RADIUS - e):
            total += product(pair_ref, i, high_ref, low_ref, block(e, -1 - i), NT)
        outer_out[e] = total


def outer_products(pair_ref, high_ref, low_ref, out_ref):
    for i in range(RADIUS):
        total = None
        for e in range(RADIUS - i):
            term = product(pair_ref, e, high_ref, low_ref, block(e, -1 - i), NN)
            total = term if total is None else total + term
        out_ref[i] = total


def inner_products(pair_ref, high_ref, low_ref, out_ref, base):
    elems = 2 * RADIUS
    for i in range(RADIUS):
        m = elems + RADIUS - 1 - i
        total = None
        for e in range(m - RADIUS, elems):
            term = product(
                pair_ref, e - RADIUS + base, high_ref, low_ref, block(e, m), NN
            )
            total = term if total is None else total + term
        out_ref[i] = total


def observe_body(
    outer0_ref, inner0_ref, outer1_ref, inner1_ref, stations_ref, weights_ref, high_ref, low_ref,
    outer_out, inner_out, readings_ref, inner_send, pair_ref, state_ref,
):
    elems, cols, dofs = state_ref.shape
    count = weights_ref.shape[0]
    section = lax.axis_index("sec")

    @pl.when(section == 0)
    def _():
        state_ref[:RADIUS] = outer0_ref[...]
        state_ref[RADIUS:] = inner0_ref[...]

    @pl.when(section != 0)
    def _():
        state_ref[:RADIUS] = outer1_ref[...]
        state_ref[RADIUS:] = inner1_ref[...]

    flat = state_ref[...].reshape(elems * cols, dofs)
    weights = weights_ref[...]
    raw = lax.dot_general(flat, weights, NT, precision=PRECISE, preferred_element_type=F32)
    local = stations_ref[...] - lax.axis_index("elem") * elems
    odd = odd_device()
    readings = jnp.zeros((cols, count), F32)
    for u in range(elems):
        here = local == jnp.where(odd, elems - 1 - u, u)
        part = jnp.where(here, raw[u * cols : (u + 1) * cols], 0.0)
        readings += part
        seen = lax.dot_general(part, weights, NN, precision=PRECISE, preferred_element_type=F32)
        if u < RADIUS:
            outer_out[u] = seen
        else:
            inner_out[u - RADIUS] = seen
            store_split(pair_ref, u - RADIUS, seen)
    readings_ref[...] = readings
    inner_products(pair_ref, high_ref, low_ref, inner_send, 0)


def seen_outer_body(value_ref, high_ref, low_ref, send_ref, pair_ref):
    for i in range(RADIUS):
        store_split(pair_ref, i, value_ref[i])
    outer_products(pair_ref, high_ref, low_ref, send_ref)


def adjoint_outer_body(total_ref, halo_ref, high_ref, low_ref, value_ref, send_ref, pair_ref):
    for i in range(RADIUS):
        value = total_ref[i] + halo_ref[i]
        value_ref[i] = value
        store_split(pair_ref, i, value)
    outer_products(pair_ref, high_ref, low_ref, send_ref)


def adjoint_inner_body(total_ref, halo_ref, high_ref, low_ref, value_ref, send_ref, pair_ref):
    for i in range(RADIUS):
        value = total_ref[i] + halo_ref[i]
        value_ref[i] = value
        store_split(pair_ref, i, value)
    inner_products(pair_ref, high_ref, low_ref, send_ref, 0)


def adjoint_local_body(outer_ref, inner_ref, high_ref, low_ref, outer_out, inner_out, pair_ref):
    elems = 2 * RADIUS
    for i in range(RADIUS):
        store_split(pair_ref, i, outer_ref[i])
        store_split(pair_ref, RADIUS + i, inner_ref[i])
    for m in range(elems):
        total = outer_ref[m] if m < RADIUS else inner_ref[m - RADIUS]
        for e in range(max(0, m - RADIUS), min(elems, m + RADIUS + 1)):
            total += product(pair_ref, e, high_ref, low_ref, block(e, m), NN)
        if m < RADIUS:
            outer_out[m] = total
        else:
            inner_out[m - RADIUS] = total


def finish_body(outer_ref, inner_ref, outer_up_ref, inner_up_ref, out_ref):
    elems, cols, half = out_ref.shape
    odd = odd_device()
    first = lax.axis_index("sec") == 0
    for u in range(elems):
        full, upper = (outer_ref, outer_up_ref) if u < RADIUS else (inner_ref, inner_up_ref)
        place = jnp.where(odd, elems - 1 - u, u)
        out_ref[place] = jnp.where(first, full[u % RADIUS, :, :half], upper[u % RADIUS])


def gram_body(stack_ref, out_ref):
    own = lax.axis_index("col")
    places = []
    for j in range(stack_ref.shape[0]):
        away = jnp.bitwise_xor(own, j)
        places.append(
            jnp.bitwise_xor(away, jnp.bitwise_and(lax.shift_right_logical(away, 1), 2))
        )
    total = None
    for core in range(stack_ref.shape[1]):
        every = jnp.concatenate([stack_ref[place, core] for place in places], axis=0)
        term = lax.dot_general(
            stack_ref[0, core], every, NT, precision=PRECISE, preferred_element_type=F32
        )
        total = term if total is None else total + term
    out_ref[...] = total


def swap(value, axis, mask):
    count = lax.axis_size(axis)
    return lax.ppermute(value, axis, [(i, i ^ mask) for i in range(count)])


def off_chip(value):
    count = lax.axis_size("elem")
    pairs = [(i, (i + (1 if i % 2 else -1)) % count) for i in range(count)]
    return lax.ppermute(value, "elem", pairs)


def on_chip(value):
    return swap(value, "elem", 1)


def after(value, *others):
    return lax.optimization_barrier((value, *others))[0]


def per_device(probes, jacobian, neighbors, stations, obs_weights):
    cols, elems, dofs = probes.shape
    elem_total = elems * lax.axis_size("elem")
    blocks = elems * NBRS
    edge = vmem((RADIUS, cols, dofs))
    count = obs_weights.shape[0]
    half = dofs // 2

    def pair(slots):
        return pltpu.VMEM((slots, 2 * cols, dofs), BF16)

    prepare = call(
        functools.partial(prepare_body, elem_total), "prepare",
        (vmem((blocks, dofs, dofs), BF16),) * 2, [IN_SMEM, IN_HBM],
        (pltpu.VMEM((elems, NBRS, dofs, dofs), F32), pltpu.SemaphoreType.DMA((elems, NBRS))),
        vmem=46 << 20, moved=2 * 10**7,
    )
    mirror = call(mirror_body, "mirror", (edge, edge), [IN_VMEM])
    tangent_near = call(
        tangent_near_body, "tangent_near", (edge, edge), [IN_VMEM] * 5, (pair(9),),
    )
    tangent_far = call(
        tangent_far_body, "tangent_far", edge, [IN_VMEM] * 4, (pair(RADIUS),)
    )
    observe = call(
        observe_body, "observe", (edge, edge, vmem((cols, count)), edge), [IN_VMEM] * 8,
        (pair(RADIUS), pltpu.VMEM((elems, cols, dofs), F32)),
    )
    adjoint_local = call(
        adjoint_local_body, "adjoint_local", (edge, edge), [IN_VMEM] * 4, (pair(elems),),
    )
    seen_products = call(
        seen_outer_body, "seen_outer", edge, [IN_VMEM] * 3, (pair(RADIUS),)
    )
    adjoint_outer = call(
        adjoint_outer_body, "adjoint_outer", (edge, edge), [IN_VMEM] * 4, (pair(RADIUS),),
    )
    adjoint_inner = call(
        adjoint_inner_body, "adjoint_inner", (edge, edge), [IN_VMEM] * 4, (pair(RADIUS),),
    )
    finish = call(
        finish_body, "finish", jax.ShapeDtypeStruct((elems, cols, half), F32), [IN_VMEM] * 4
    )
    col_count = lax.axis_size("col")
    gram_part = call(gram_body, "gram_part", vmem((cols, cols * col_count)), [IN_VMEM])

    def tangent(outer, inner, high, low):
        for _ in range(STEPS):
            inner_in = on_chip(inner)
            outer_in = off_chip(outer)
            outer, inner = tangent_near(outer, inner, inner_in, high, low)
            outer = tangent_far(outer, outer_in, high, low)
        return outer, inner

    def to_next(outer, inner):
        inner = lax.ppermute(inner, "sec", [(0, 1)])
        return lax.ppermute(outer, "sec", [(0, 1)]), inner

    high, low = prepare(neighbors, jacobian)
    state0 = tangent(*mirror(jnp.transpose(probes, (1, 0, 2))), high, low)
    state1 = tangent(*to_next(*state0), high, low)
    seen_outer, seen_inner, readings, inner_send = observe(
        *state0, *state1, stations.reshape(1, count), obs_weights, high, low
    )

    def gather(stack, mask, *others):
        return jnp.concatenate([stack, swap(after(stack, *others), "col", mask)], axis=0)

    inner_in = on_chip(inner_send)
    stack = jnp.stack([readings, on_chip(readings)])[None]
    outer_in = off_chip(seen_products(seen_outer, high, low))
    outer, inner = adjoint_local(seen_outer, seen_inner, high, low)
    inner, inner_send = adjoint_inner(inner, inner_in, high, low)
    inner_in = on_chip(inner_send)
    stack = gather(stack, 1, inner_in)
    outer, outer_send = adjoint_outer(after(outer, inner_in), outer_in, high, low)
    outer_in = off_chip(outer_send)
    outer, inner = adjoint_local(outer, inner, high, low)
    inner = inner + inner_in
    inner_back = lax.ppermute(after(inner, outer_in), "sec", [(1, 0)])
    stack = gather(stack, 2, inner)
    outer = after(outer, inner) + outer_in
    outer_back = lax.ppermute(outer, "sec", [(1, 0)])
    stack = gather(stack, 6, outer)
    inner, inner_send = adjoint_inner(seen_inner, inner_back, high, low)
    inner_in = on_chip(inner_send)
    gram = gram_part(stack)
    gram = gram + swap(gram, "elem", 2)
    outer, outer_send = adjoint_outer(after(seen_outer, inner_send), outer_back, high, low)
    outer_in = off_chip(outer_send)
    outer, inner = adjoint_local(outer, inner, high, low)
    inner, inner_send = adjoint_inner(inner, inner_in, high, low)
    inner_in = on_chip(inner_send)
    gram = gram + swap(after(gram, inner_in), "elem", 4)
    outer, outer_send = adjoint_outer(after(outer, inner_in), outer_in, high, low)
    outer_in = off_chip(outer_send)
    outer, inner = adjoint_local(outer, inner, high, low)
    inner = inner + inner_in
    inner_up = lax.ppermute(after(inner, outer_in)[:, :, half:], "sec", [(0, 1)])
    gram = gram + swap(after(gram, outer_in), "elem", 12)
    outer = after(outer, inner) + outer_in
    outer_up = lax.ppermute(outer[:, :, half:], "sec", [(0, 1)])
    gram = gram + swap(after(gram, outer), "sec", 1)
    hess = jnp.transpose(finish(outer, inner, outer_up, inner_up), (1, 0, 2))
    return hess, gram * (1.0 / (elem_total * dofs))


def solution(mesh):
    in_specs = (
        P("col", "elem", None),
        P("sec", "elem", None, None, None),
        P("elem", None),
        P("elem"),
        P("elem", None),
    )
    out_specs = (P("col", "elem", "sec"), P("col", None))
    return jax.shard_map(
        per_device, mesh=mesh, in_specs=in_specs, out_specs=out_specs, check_vma=False
    )
```

```python
import functools

import jax
import jax.numpy as jnp
from jax import lax
from jax.experimental import pallas as pl
from jax.experimental.pallas import tpu as pltpu
from jax.sharding import PartitionSpec as P

NBRS = 7
RADIUS = 3
STEPS = 2
WORK = {
    "prepare": 30,
    "mirror": 30,
    "tangent_near": 30,
    "tangent_far": 30,
    "observe": 200,
    "adjoint_local": 100,
    "adjoint_outer": 400,
    "adjoint_inner": 100,
    "seen_outer": 100,
    "finish": 1000,
    "gram_part": 30,
}
PRECISE = lax.Precision.HIGHEST
BF16 = jnp.bfloat16
F32 = jnp.float32
NN = (((1,), (0,)), ((), ()))
NT = (((1,), (1,)), ((), ()))

IN_VMEM = pl.BlockSpec(memory_space=pltpu.VMEM)
IN_SMEM = pl.BlockSpec(memory_space=pltpu.SMEM)
IN_HBM = pl.BlockSpec(memory_space=pltpu.HBM)


def call(body, name, outs, in_specs, scratch=(), vmem=4 << 20, moved=10**5):
    single = not isinstance(outs, tuple)
    return pl.pallas_call(
        body,
        name=name,
        out_shape=outs,
        in_specs=in_specs,
        out_specs=IN_VMEM if single else (IN_VMEM,) * len(outs),
        scratch_shapes=list(scratch),
        compiler_params=pltpu.CompilerParams(vmem_limit_bytes=vmem),
        cost_estimate=pl.CostEstimate(flops=WORK[name] * 10**7, bytes_accessed=moved, transcendentals=0),
    )


def vmem(shape, dtype=F32):
    return pltpu.VMEM(shape, dtype)


def split(value):
    high = value.astype(BF16)
    low = (value - high.astype(F32)).astype(BF16)
    return high, low


def store_split(pair_ref, slot, value):
    rows = value.shape[0]
    high, low = split(value)
    pair_ref[slot, :rows] = high
    pair_ref[slot, rows:] = low


def product(pair_ref, slot, high_ref, low_ref, block, dims):
    rows = pair_ref.shape[1] // 2
    both = lax.dot_general(pair_ref[slot], high_ref[block], dims, preferred_element_type=F32)
    rest = lax.dot_general(
        pair_ref[slot, :rows], low_ref[block], dims, preferred_element_type=F32
    )
    return both[:rows] + both[rows:] + rest


def odd_device():
    return lax.rem(lax.axis_index("elem"), 2) == 1


def prepare_body(elem_total, nbr_ref, jac_ref, high_ref, low_ref, buffer, sems):
    elems = buffer.shape[0]
    copies = [
        [
            pltpu.make_async_copy(jac_ref.at[0, e, k], buffer.at[e, k], sems.at[e, k])
            for k in range(NBRS)
        ]
        for e in range(elems)
    ]
    for row in copies:
        for copy in row:
            copy.start()
    first = lax.axis_index("elem") * elems
    odd = odd_device()
    for e in range(elems):
        for k in range(NBRS):
            copies[e][k].wait()
            offset = lax.rem(nbr_ref[e, k] - (first + e) + RADIUS + elem_total, elem_total)
            slot = e * NBRS + offset
            slot = jnp.where(odd, elems * NBRS - 1 - slot, slot)
            high, low = split(buffer[e, k])
            high_ref[slot] = high
            low_ref[slot] = low


def mirror_body(field_ref, outer_ref, inner_ref):
    elems = field_ref.shape[0]
    odd = odd_device()
    for i in range(RADIUS):
        outer_ref[i] = field_ref[jnp.where(odd, elems - 1 - i, i)]
        inner_ref[i] = field_ref[jnp.where(odd, elems - 1 - RADIUS - i, RADIUS + i)]


def block(e, m):
    return e * NBRS + m - e + RADIUS


def tangent_near_body(
    outer_ref, inner_ref, halo_ref, high_ref, low_ref, outer_out, inner_out, pair_ref
):
    elems = 2 * RADIUS
    for i in range(RADIUS):
        store_split(pair_ref, i, outer_ref[i])
        store_split(pair_ref, RADIUS + i, inner_ref[i])
        store_split(pair_ref, elems + RADIUS - 1 - i, halo_ref[i])
    for e in range(elems):
        total = outer_ref[e] if e < RADIUS else inner_ref[e - RADIUS]
        for m in range(max(0, e - RADIUS), e + RADIUS + 1):
            total += product(pair_ref, m, high_ref, low_ref, block(e, m), NT)
        if e < RADIUS:
            outer_out[e] = total
        else:
            inner_out[e - RADIUS] = total


def tangent_far_body(outer_ref, halo_ref, high_ref, low_ref, outer_out, pair_ref):
    for i in range(RADIUS):
        store_split(pair_ref, i, halo_ref[i])
    for e in range(RADIUS):
        total = outer_ref[e]
        for i in range(RADIUS - e):
            total += product(pair_ref, i, high_ref, low_ref, block(e, -1 - i), NT)
        outer_out[e] = total


def outer_products(pair_ref, high_ref, low_ref, out_ref):
    for i in range(RADIUS):
        total = None
        for e in range(RADIUS - i):
            term = product(pair_ref, e, high_ref, low_ref, block(e, -1 - i), NN)
            total = term if total is None else total + term
        out_ref[i] = total


def inner_products(pair_ref, high_ref, low_ref, out_ref, base):
    elems = 2 * RADIUS
    for i in range(RADIUS):
        m = elems + RADIUS - 1 - i
        total = None
        for e in range(m - RADIUS, elems):
            term = product(
                pair_ref, e - RADIUS + base, high_ref, low_ref, block(e, m), NN
            )
            total = term if total is None else total + term
        out_ref[i] = total


def observe_body(
    outer0_ref, inner0_ref, outer1_ref, inner1_ref, stations_ref, weights_ref, high_ref, low_ref,
    outer_out, inner_out, readings_ref, inner_send, pair_ref, state_ref,
):
    elems, cols, dofs = state_ref.shape
    count = weights_ref.shape[0]
    section = lax.axis_index("sec")

    @pl.when(section == 0)
    def _():
        state_ref[:RADIUS] = outer0_ref[...]
        state_ref[RADIUS:] = inner0_ref[...]

    @pl.when(section != 0)
    def _():
        state_ref[:RADIUS] = outer1_ref[...]
        state_ref[RADIUS:] = inner1_ref[...]

    flat = state_ref[...].reshape(elems * cols, dofs)
    weights = weights_ref[...]
    raw = lax.dot_general(flat, weights, NT, precision=PRECISE, preferred_element_type=F32)
    local = stations_ref[...] - lax.axis_index("elem") * elems
    odd = odd_device()
    readings = jnp.zeros((cols, count), F32)
    for u in range(elems):
        here = local == jnp.where(odd, elems - 1 - u, u)
        part = jnp.where(here, raw[u * cols : (u + 1) * cols], 0.0)
        readings += part
        seen = lax.dot_general(part, weights, NN, precision=PRECISE, preferred_element_type=F32)
        if u < RADIUS:
            outer_out[u] = seen
        else:
            inner_out[u - RADIUS] = seen
            store_split(pair_ref, u - RADIUS, seen)
    readings_ref[...] = readings
    inner_products(pair_ref, high_ref, low_ref, inner_send, 0)


def seen_outer_body(value_ref, high_ref, low_ref, send_ref, pair_ref):
    for i in range(RADIUS):
        store_split(pair_ref, i, value_ref[i])
    outer_products(pair_ref, high_ref, low_ref, send_ref)


def adjoint_outer_body(total_ref, halo_ref, high_ref, low_ref, value_ref, send_ref, pair_ref):
    for i in range(RADIUS):
        value = total_ref[i] + halo_ref[i]
        value_ref[i] = value
        store_split(pair_ref, i, value)
    outer_products(pair_ref, high_ref, low_ref, send_ref)


def adjoint_inner_body(total_ref, halo_ref, high_ref, low_ref, value_ref, send_ref, pair_ref):
    for i in range(RADIUS):
        value = total_ref[i] + halo_ref[i]
        value_ref[i] = value
        store_split(pair_ref, i, value)
    inner_products(pair_ref, high_ref, low_ref, send_ref, 0)


def adjoint_local_body(outer_ref, inner_ref, high_ref, low_ref, outer_out, inner_out, pair_ref):
    elems = 2 * RADIUS
    for i in range(RADIUS):
        store_split(pair_ref, i, outer_ref[i])
        store_split(pair_ref, RADIUS + i, inner_ref[i])
    for m in range(elems):
        total = outer_ref[m] if m < RADIUS else inner_ref[m - RADIUS]
        for e in range(max(0, m - RADIUS), min(elems, m + RADIUS + 1)):
            total += product(pair_ref, e, high_ref, low_ref, block(e, m), NN)
        if m < RADIUS:
            outer_out[m] = total
        else:
            inner_out[m - RADIUS] = total


def finish_body(scale, field_ref, upper_ref, gram_ref, rest_ref, out_ref, gram_out):
    elems, cols, half = out_ref.shape
    odd = odd_device()
    first = lax.axis_index("sec") == 0
    for u in range(elems):
        place = jnp.where(odd, elems - 1 - u, u)
        out_ref[place] = jnp.where(first, field_ref[u, :, :half], upper_ref[u])
    gram_out[...] = (gram_ref[...] + rest_ref[...]) * scale


def gram_body(stack_ref, out_ref):
    own = lax.axis_index("col")
    places = []
    for j in range(stack_ref.shape[0]):
        away = jnp.bitwise_xor(own, j)
        places.append(
            jnp.bitwise_xor(away, jnp.bitwise_and(lax.shift_right_logical(away, 1), 2))
        )
    total = None
    for core in range(stack_ref.shape[1]):
        every = jnp.concatenate([stack_ref[place, core] for place in places], axis=0)
        term = lax.dot_general(
            stack_ref[0, core], every, NT, precision=PRECISE, preferred_element_type=F32
        )
        total = term if total is None else total + term
    out_ref[...] = total


def swap(value, axis, mask):
    count = lax.axis_size(axis)
    return lax.ppermute(value, axis, [(i, i ^ mask) for i in range(count)])


def off_chip(value):
    count = lax.axis_size("elem")
    pairs = [(i, (i + (1 if i % 2 else -1)) % count) for i in range(count)]
    return lax.ppermute(value, "elem", pairs)


def on_chip(value):
    return swap(value, "elem", 1)


def after(value, *others):
    return lax.optimization_barrier((value, *others))[0]


def per_device(probes, jacobian, neighbors, stations, obs_weights):
    cols, elems, dofs = probes.shape
    elem_total = elems * lax.axis_size("elem")
    blocks = elems * NBRS
    edge = vmem((RADIUS, cols, dofs))
    count = obs_weights.shape[0]
    half = dofs // 2
    col_count = lax.axis_size("col")

    def pair(slots):
        return pltpu.VMEM((slots, 2 * cols, dofs), BF16)

    prepare = call(
        functools.partial(prepare_body, elem_total), "prepare",
        (vmem((blocks, dofs, dofs), BF16),) * 2, [IN_SMEM, IN_HBM],
        (pltpu.VMEM((elems, NBRS, dofs, dofs), F32), pltpu.SemaphoreType.DMA((elems, NBRS))),
        vmem=46 << 20, moved=2 * 10**7,
    )
    mirror = call(mirror_body, "mirror", (edge, edge), [IN_VMEM])
    tangent_near = call(
        tangent_near_body, "tangent_near", (edge, edge), [IN_VMEM] * 5, (pair(9),),
    )
    tangent_far = call(
        tangent_far_body, "tangent_far", edge, [IN_VMEM] * 4, (pair(RADIUS),)
    )
    observe = call(
        observe_body, "observe", (edge, edge, vmem((cols, count)), edge), [IN_VMEM] * 8,
        (pair(RADIUS), pltpu.VMEM((elems, cols, dofs), F32)),
    )
    adjoint_local = call(
        adjoint_local_body, "adjoint_local", (edge, edge), [IN_VMEM] * 4, (pair(elems),),
    )
    seen_products = call(
        seen_outer_body, "seen_outer", edge, [IN_VMEM] * 3, (pair(RADIUS),)
    )
    adjoint_outer = call(
        adjoint_outer_body, "adjoint_outer", (edge, edge), [IN_VMEM] * 4, (pair(RADIUS),),
    )
    adjoint_inner = call(
        adjoint_inner_body, "adjoint_inner", (edge, edge), [IN_VMEM] * 4, (pair(RADIUS),),
    )
    finish = call(
        functools.partial(finish_body, 1.0 / (elem_total * dofs)), "finish",
        (
            jax.ShapeDtypeStruct((elems, cols, half), F32),
            jax.ShapeDtypeStruct((cols, cols * col_count), F32),
        ),
        [IN_VMEM] * 4,
    )
    gram_part = call(gram_body, "gram_part", vmem((cols, cols * col_count)), [IN_VMEM])

    def tangent(outer, inner, high, low):
        for _ in range(STEPS):
            inner_in = on_chip(inner)
            outer_in = off_chip(outer)
            outer, inner = tangent_near(outer, inner, inner_in, high, low)
            outer = tangent_far(outer, outer_in, high, low)
        return outer, inner

    def to_next(outer, inner):
        inner = lax.ppermute(inner, "sec", [(0, 1)])
        return lax.ppermute(outer, "sec", [(0, 1)]), inner

    high, low = prepare(neighbors, jacobian)
    state0 = tangent(*mirror(jnp.transpose(probes, (1, 0, 2))), high, low)
    state1 = tangent(*to_next(*state0), high, low)
    seen_outer, seen_inner, readings, inner_send = observe(
        *state0, *state1, stations.reshape(1, count), obs_weights, high, low
    )

    def gather(stack, mask, *others):
        return jnp.concatenate([stack, swap(after(stack, *others), "col", mask)], axis=0)

    inner_in = on_chip(inner_send)
    stack = jnp.stack([readings, on_chip(readings)])[None]
    outer_in = off_chip(seen_products(seen_outer, high, low))
    outer, inner = adjoint_local(seen_outer, seen_inner, high, low)
    inner, inner_send = adjoint_inner(inner, inner_in, high, low)
    inner_in = on_chip(inner_send)
    stack = gather(stack, 1, inner_in)
    outer, outer_send = adjoint_outer(after(outer, inner_in), outer_in, high, low)
    outer_in = off_chip(outer_send)
    outer, inner = adjoint_local(outer, inner, high, low)
    inner = inner + inner_in
    inner_back = lax.ppermute(after(inner, outer_in), "sec", [(1, 0)])
    stack = gather(stack, 2, inner)
    outer = after(outer, inner) + outer_in
    outer_back = lax.ppermute(outer, "sec", [(1, 0)])
    stack = gather(stack, 6, outer)
    inner, inner_send = adjoint_inner(seen_inner, inner_back, high, low)
    inner_in = on_chip(inner_send)
    gram = gram_part(stack)
    gram = gram + swap(gram, "elem", 2)
    outer, outer_send = adjoint_outer(after(seen_outer, inner_send), outer_back, high, low)
    outer_in = off_chip(outer_send)
    outer, inner = adjoint_local(outer, inner, high, low)
    inner, inner_send = adjoint_inner(inner, inner_in, high, low)
    inner_in = on_chip(inner_send)
    gram = gram + swap(after(gram, inner_in), "elem", 4)
    outer, outer_send = adjoint_outer(after(outer, inner_in), outer_in, high, low)
    outer_in = off_chip(outer_send)
    outer, inner = adjoint_local(outer, inner, high, low)
    inner = inner + inner_in
    gram = gram + swap(after(gram, outer_in), "elem", 12)
    outer = after(outer, inner) + outer_in
    field = jnp.concatenate([outer, inner])
    upper = lax.ppermute(field[:, :, half:], "sec", [(0, 1)])
    hess, gram = finish(field, upper, gram, swap(gram, "sec", 1))
    return jnp.transpose(hess, (1, 0, 2)), gram


def solution(mesh):
    in_specs = (
        P("col", "elem", None),
        P("sec", "elem", None, None, None),
        P("elem", None),
        P("elem"),
        P("elem", None),
    )
    out_specs = (P("col", "elem", "sec"), P("col", None))
    return jax.shard_map(
        per_device, mesh=mesh, in_specs=in_specs, out_specs=out_specs, check_vma=False
    )
```

```python
import functools

import jax
import jax.numpy as jnp
from jax import lax
from jax.experimental import pallas as pl
from jax.experimental.pallas import tpu as pltpu
from jax.sharding import PartitionSpec as P

NBRS = 7
RADIUS = 3
STEPS = 2
WORK = {
    "prepare": 30,
    "mirror": 30,
    "tangent_near": 30,
    "tangent_far": 30,
    "observe": 200,
    "adjoint_local": 100,
    "adjoint_outer": 400,
    "adjoint_inner": 100,
    "seen_outer": 100,
    "finish": 1000,
    "gram_part": 30,
}
PRECISE = lax.Precision.HIGHEST
BF16 = jnp.bfloat16
F32 = jnp.float32
NN = (((1,), (0,)), ((), ()))
NT = (((1,), (1,)), ((), ()))

IN_VMEM = pl.BlockSpec(memory_space=pltpu.VMEM)
IN_SMEM = pl.BlockSpec(memory_space=pltpu.SMEM)
IN_HBM = pl.BlockSpec(memory_space=pltpu.HBM)


def call(body, name, outs, in_specs, scratch=(), vmem=4 << 20, moved=10**5):
    single = not isinstance(outs, tuple)
    return pl.pallas_call(
        body,
        name=name,
        out_shape=outs,
        in_specs=in_specs,
        out_specs=IN_VMEM if single else (IN_VMEM,) * len(outs),
        scratch_shapes=list(scratch),
        compiler_params=pltpu.CompilerParams(vmem_limit_bytes=vmem),
        cost_estimate=pl.CostEstimate(flops=WORK[name] * 10**7, bytes_accessed=moved, transcendentals=0),
    )


def vmem(shape, dtype=F32):
    return pltpu.VMEM(shape, dtype)


def split(value):
    high = value.astype(BF16)
    low = (value - high.astype(F32)).astype(BF16)
    return high, low


def store_split(pair_ref, slot, value):
    rows = value.shape[0]
    high, low = split(value)
    pair_ref[slot, :rows] = high
    pair_ref[slot, rows:] = low


def product(pair_ref, slot, high_ref, low_ref, block, dims):
    rows = pair_ref.shape[1] // 2
    both = lax.dot_general(pair_ref[slot], high_ref[block], dims, preferred_element_type=F32)
    rest = lax.dot_general(
        pair_ref[slot, :rows], low_ref[block], dims, preferred_element_type=F32
    )
    return both[:rows] + both[rows:] + rest


def odd_device():
    return lax.rem(lax.axis_index("elem"), 2) == 1


def prepare_body(elem_total, nbr_ref, jac_ref, high_ref, low_ref, buffer, sems):
    elems = buffer.shape[0]
    copies = [
        [
            pltpu.make_async_copy(jac_ref.at[0, e, k], buffer.at[e, k], sems.at[e, k])
            for k in range(NBRS)
        ]
        for e in range(elems)
    ]
    for row in copies:
        for copy in row:
            copy.start()
    first = lax.axis_index("elem") * elems
    odd = odd_device()
    for e in range(elems):
        for k in range(NBRS):
            copies[e][k].wait()
            offset = lax.rem(nbr_ref[e, k] - (first + e) + RADIUS + elem_total, elem_total)
            slot = e * NBRS + offset
            slot = jnp.where(odd, elems * NBRS - 1 - slot, slot)
            high, low = split(buffer[e, k])
            high_ref[slot] = high
            low_ref[slot] = low


def mirror_body(field_ref, outer_ref, inner_ref):
    elems = field_ref.shape[0]
    odd = odd_device()
    for i in range(RADIUS):
        outer_ref[i] = field_ref[jnp.where(odd, elems - 1 - i, i)]
        inner_ref[i] = field_ref[jnp.where(odd, elems - 1 - RADIUS - i, RADIUS + i)]


def only(section, copies, body):
    def guarded(*refs):
        active = lax.axis_index("sec") == section

        @pl.when(active)
        def _():
            body(*refs)

        @pl.when(jnp.logical_not(active))
        def _():
            for source, target in copies:
                refs[target][...] = refs[source][...]

    return guarded


def block(e, m):
    return e * NBRS + m - e + RADIUS


def tangent_near_body(
    outer_ref, inner_ref, halo_ref, high_ref, low_ref, outer_out, inner_out, pair_ref
):
    elems = 2 * RADIUS
    for i in range(RADIUS):
        store_split(pair_ref, i, outer_ref[i])
        store_split(pair_ref, RADIUS + i, inner_ref[i])
        store_split(pair_ref, elems + RADIUS - 1 - i, halo_ref[i])
    for e in range(elems):
        total = outer_ref[e] if e < RADIUS else inner_ref[e - RADIUS]
        for m in range(max(0, e - RADIUS), e + RADIUS + 1):
            total += product(pair_ref, m, high_ref, low_ref, block(e, m), NT)
        if e < RADIUS:
            outer_out[e] = total
        else:
            inner_out[e - RADIUS] = total


def tangent_far_body(outer_ref, halo_ref, high_ref, low_ref, outer_out, pair_ref):
    for i in range(RADIUS):
        store_split(pair_ref, i, halo_ref[i])
    for e in range(RADIUS):
        total = outer_ref[e]
        for i in range(RADIUS - e):
            total += product(pair_ref, i, high_ref, low_ref, block(e, -1 - i), NT)
        outer_out[e] = total


def outer_products(pair_ref, high_ref, low_ref, out_ref):
    for i in range(RADIUS):
        total = None
        for e in range(RADIUS - i):
            term = product(pair_ref, e, high_ref, low_ref, block(e, -1 - i), NN)
            total = term if total is None else total + term
        out_ref[i] = total


def inner_products(pair_ref, high_ref, low_ref, out_ref, base):
    elems = 2 * RADIUS
    for i in range(RADIUS):
        m = elems + RADIUS - 1 - i
        total = None
        for e in range(m - RADIUS, elems):
            term = product(
                pair_ref, e - RADIUS + base, high_ref, low_ref, block(e, m), NN
            )
            total = term if total is None else total + term
        out_ref[i] = total


def observe_body(
    outer0_ref, inner0_ref, outer1_ref, inner1_ref, stations_ref, weights_ref, high_ref, low_ref,
    outer_out, inner_out, readings_ref, inner_send, pair_ref, state_ref,
):
    elems, cols, dofs = state_ref.shape
    count = weights_ref.shape[0]
    section = lax.axis_index("sec")

    @pl.when(section == 0)
    def _():
        state_ref[:RADIUS] = outer0_ref[...]
        state_ref[RADIUS:] = inner0_ref[...]

    @pl.when(section != 0)
    def _():
        state_ref[:RADIUS] = outer1_ref[...]
        state_ref[RADIUS:] = inner1_ref[...]

    flat = state_ref[...].reshape(elems * cols, dofs)
    weights = weights_ref[...]
    raw = lax.dot_general(flat, weights, NT, precision=PRECISE, preferred_element_type=F32)
    local = stations_ref[...] - lax.axis_index("elem") * elems
    odd = odd_device()
    readings = jnp.zeros((cols, count), F32)
    parts = []
    for u in range(elems):
        here = local == jnp.where(odd, elems - 1 - u, u)
        part = jnp.where(here, raw[u * cols : (u + 1) * cols], 0.0)
        readings += part
        parts.append(part)
    every = lax.dot_general(
        jnp.concatenate(parts, axis=0), weights, NN, precision=PRECISE, preferred_element_type=F32
    )
    for u in range(elems):
        seen = every[u * cols : (u + 1) * cols]
        if u < RADIUS:
            outer_out[u] = seen
        else:
            inner_out[u - RADIUS] = seen
            store_split(pair_ref, u - RADIUS, seen)
    readings_ref[...] = readings
    inner_products(pair_ref, high_ref, low_ref, inner_send, 0)


def seen_outer_body(value_ref, high_ref, low_ref, send_ref, pair_ref):
    for i in range(RADIUS):
        store_split(pair_ref, i, value_ref[i])
    outer_products(pair_ref, high_ref, low_ref, send_ref)


def adjoint_outer_body(total_ref, halo_ref, high_ref, low_ref, value_ref, send_ref, pair_ref):
    for i in range(RADIUS):
        value = total_ref[i] + halo_ref[i]
        value_ref[i] = value
        store_split(pair_ref, i, value)
    outer_products(pair_ref, high_ref, low_ref, send_ref)


def adjoint_inner_body(total_ref, halo_ref, high_ref, low_ref, value_ref, send_ref, pair_ref):
    for i in range(RADIUS):
        value = total_ref[i] + halo_ref[i]
        value_ref[i] = value
        store_split(pair_ref, i, value)
    inner_products(pair_ref, high_ref, low_ref, send_ref, 0)


def adjoint_local_body(outer_ref, inner_ref, high_ref, low_ref, outer_out, inner_out, pair_ref):
    elems = 2 * RADIUS
    for i in range(RADIUS):
        store_split(pair_ref, i, outer_ref[i])
        store_split(pair_ref, RADIUS + i, inner_ref[i])
    for m in range(elems):
        total = outer_ref[m] if m < RADIUS else inner_ref[m - RADIUS]
        for e in range(max(0, m - RADIUS), min(elems, m + RADIUS + 1)):
            total += product(pair_ref, e, high_ref, low_ref, block(e, m), NN)
        if m < RADIUS:
            outer_out[m] = total
        else:
            inner_out[m - RADIUS] = total


def finish_body(scale, field_ref, upper_ref, gram_ref, rest_ref, out_ref, gram_out):
    elems, cols, half = out_ref.shape
    odd = odd_device()
    first = lax.axis_index("sec") == 0
    for u in range(elems):
        place = jnp.where(odd, elems - 1 - u, u)
        out_ref[place] = jnp.where(first, field_ref[u, :, :half], upper_ref[u])
    gram_out[...] = (gram_ref[...] + rest_ref[...]) * scale


def gram_body(stack_ref, out_ref):
    own = lax.axis_index("col")
    places = []
    for j in range(stack_ref.shape[0]):
        away = jnp.bitwise_xor(own, j)
        places.append(
            jnp.bitwise_xor(away, jnp.bitwise_and(lax.shift_right_logical(away, 1), 2))
        )
    total = None
    for core in range(stack_ref.shape[1]):
        every = jnp.concatenate([stack_ref[place, core] for place in places], axis=0)
        term = lax.dot_general(
            stack_ref[0, core], every, NT, precision=PRECISE, preferred_element_type=F32
        )
        total = term if total is None else total + term
    out_ref[...] = total


def swap(value, axis, mask):
    count = lax.axis_size(axis)
    return lax.ppermute(value, axis, [(i, i ^ mask) for i in range(count)])


def off_chip(value):
    count = lax.axis_size("elem")
    pairs = [(i, (i + (1 if i % 2 else -1)) % count) for i in range(count)]
    return lax.ppermute(value, "elem", pairs)


def on_chip(value):
    return swap(value, "elem", 1)


def after(value, *others):
    return lax.optimization_barrier((value, *others))[0]


def per_device(probes, jacobian, neighbors, stations, obs_weights):
    cols, elems, dofs = probes.shape
    elem_total = elems * lax.axis_size("elem")
    blocks = elems * NBRS
    edge = vmem((RADIUS, cols, dofs))
    count = obs_weights.shape[0]
    half = dofs // 2
    col_count = lax.axis_size("col")

    def pair(slots):
        return pltpu.VMEM((slots, 2 * cols, dofs), BF16)

    prepare = call(
        functools.partial(prepare_body, elem_total), "prepare",
        (vmem((blocks, dofs, dofs), BF16),) * 2, [IN_SMEM, IN_HBM],
        (pltpu.VMEM((elems, NBRS, dofs, dofs), F32), pltpu.SemaphoreType.DMA((elems, NBRS))),
        vmem=46 << 20, moved=2 * 10**7,
    )
    mirror = call(mirror_body, "mirror", (edge, edge), [IN_VMEM])
    def make_tangent_near(body):
        return call(
            body, "tangent_near", (edge, edge), [IN_VMEM] * 5, (pair(9),),
        )

    tangent_near = make_tangent_near(tangent_near_body)
    tangent_near_first = make_tangent_near(only(0, ((0, 5), (1, 6)), tangent_near_body))
    def make_tangent_far(body):
        return call(
            body, "tangent_far", edge, [IN_VMEM] * 4, (pair(RADIUS),)
        )

    tangent_far = make_tangent_far(tangent_far_body)
    tangent_far_first = make_tangent_far(only(0, ((0, 4),), tangent_far_body))
    observe = call(
        observe_body, "observe", (edge, edge, vmem((cols, count)), edge), [IN_VMEM] * 8,
        (pair(RADIUS), pltpu.VMEM((elems, cols, dofs), F32)),
    )
    def make_adjoint_local(body):
        return call(
            body, "adjoint_local", (edge, edge), [IN_VMEM] * 4, (pair(elems),),
        )

    adjoint_local = make_adjoint_local(adjoint_local_body)
    adjoint_local_last = make_adjoint_local(only(0, ((0, 4), (1, 5)), adjoint_local_body))
    seen_products = call(
        seen_outer_body, "seen_outer", edge, [IN_VMEM] * 3, (pair(RADIUS),)
    )
    def make_adjoint_outer(body):
        return call(
            body, "adjoint_outer", (edge, edge), [IN_VMEM] * 4, (pair(RADIUS),),
        )

    adjoint_outer = make_adjoint_outer(adjoint_outer_body)
    adjoint_outer_last = make_adjoint_outer(only(0, ((0, 4), (1, 5)), adjoint_outer_body))
    def make_adjoint_inner(body):
        return call(
            body, "adjoint_inner", (edge, edge), [IN_VMEM] * 4, (pair(RADIUS),),
        )

    adjoint_inner = make_adjoint_inner(adjoint_inner_body)
    adjoint_inner_last = make_adjoint_inner(only(0, ((0, 4), (1, 5)), adjoint_inner_body))
    finish = call(
        functools.partial(finish_body, 1.0 / (elem_total * dofs)), "finish",
        (
            jax.ShapeDtypeStruct((elems, cols, half), F32),
            jax.ShapeDtypeStruct((cols, cols * col_count), F32),
        ),
        [IN_VMEM] * 4,
    )
    gram_part = call(gram_body, "gram_part", vmem((cols, cols * col_count)), [IN_VMEM])

    def tangent(outer, inner, high, low, near, far):
        for _ in range(STEPS):
            inner_in = on_chip(inner)
            outer_in = off_chip(outer)
            outer, inner = near(outer, inner, inner_in, high, low)
            outer = far(outer, outer_in, high, low)
        return outer, inner

    def to_next(outer, inner):
        inner = lax.ppermute(inner, "sec", [(0, 1)])
        return lax.ppermute(outer, "sec", [(0, 1)]), inner

    high, low = prepare(neighbors, jacobian)
    start = mirror(jnp.transpose(probes, (1, 0, 2)))
    state0 = tangent(*start, high, low, tangent_near_first, tangent_far_first)
    state1 = tangent(*to_next(*state0), high, low, tangent_near, tangent_far)
    seen_outer, seen_inner, readings, inner_send = observe(
        *state0, *state1, stations.reshape(1, count), obs_weights, high, low
    )

    def gather(stack, mask, *others):
        return jnp.concatenate([stack, swap(after(stack, *others), "col", mask)], axis=0)

    inner_in = on_chip(inner_send)
    stack = jnp.stack([readings, on_chip(readings)])[None]
    outer_in = off_chip(seen_products(seen_outer, high, low))
    outer, inner = adjoint_local(seen_outer, seen_inner, high, low)
    inner, inner_send = adjoint_inner(inner, inner_in, high, low)
    inner_in = on_chip(inner_send)
    stack = gather(stack, 1, inner_in)
    outer, outer_send = adjoint_outer(after(outer, inner_in), outer_in, high, low)
    outer_in = off_chip(outer_send)
    outer, inner = adjoint_local(outer, inner, high, low)
    inner = inner + inner_in
    inner_back = lax.ppermute(after(inner, outer_in), "sec", [(1, 0)])
    stack = gather(stack, 2, inner)
    outer = after(outer, inner) + outer_in
    outer_back = lax.ppermute(outer, "sec", [(1, 0)])
    stack = gather(stack, 6, outer)
    inner, inner_send = adjoint_inner_last(seen_inner, inner_back, high, low)
    inner_in = on_chip(inner_send)
    gram = gram_part(stack)
    gram = gram + swap(gram, "elem", 2)
    outer, outer_send = adjoint_outer_last(after(seen_outer, inner_send), outer_back, high, low)
    outer_in = off_chip(outer_send)
    outer, inner = adjoint_local_last(outer, inner, high, low)
    inner, inner_send = adjoint_inner_last(inner, inner_in, high, low)
    inner_in = on_chip(inner_send)
    gram = gram + swap(after(gram, inner_in), "elem", 4)
    outer, outer_send = adjoint_outer_last(after(outer, inner_in), outer_in, high, low)
    outer_in = off_chip(outer_send)
    outer, inner = adjoint_local_last(outer, inner, high, low)
    inner = inner + inner_in
    gram = gram + swap(after(gram, outer_in), "elem", 12)
    outer = after(outer, inner) + outer_in
    field = jnp.concatenate([outer, inner])
    upper = lax.ppermute(field[:, :, half:], "sec", [(0, 1)])
    hess, gram = finish(field, upper, gram, swap(gram, "sec", 1))
    return jnp.transpose(hess, (1, 0, 2)), gram


def solution(mesh):
    in_specs = (
        P("col", "elem", None),
        P("sec", "elem", None, None, None),
        P("elem", None),
        P("elem"),
        P("elem", None),
    )
    out_specs = (P("col", "elem", "sec"), P("col", None))
    return jax.shard_map(
        per_device, mesh=mesh, in_specs=in_specs, out_specs=out_specs, check_vma=False
    )
```

```python
import functools

import jax
import jax.numpy as jnp
from jax import lax
from jax.experimental import pallas as pl
from jax.experimental.pallas import tpu as pltpu
from jax.sharding import PartitionSpec as P

NBRS = 7
RADIUS = 3
STEPS = 2
WORK = {
    "prepare": 30,
    "mirror": 30,
    "tangent_near": 30,
    "tangent_far": 30,
    "observe": 200,
    "adjoint_local": 100,
    "adjoint_outer": 400,
    "adjoint_inner": 100,
    "seen_outer": 100,
    "finish": 1000,
    "gram_part": 30,
}
PRECISE = lax.Precision.HIGHEST
BF16 = jnp.bfloat16
F32 = jnp.float32
NN = (((1,), (0,)), ((), ()))
NT = (((1,), (1,)), ((), ()))

IN_VMEM = pl.BlockSpec(memory_space=pltpu.VMEM)
IN_SMEM = pl.BlockSpec(memory_space=pltpu.SMEM)
IN_HBM = pl.BlockSpec(memory_space=pltpu.HBM)


def call(body, name, outs, in_specs, scratch=(), vmem=4 << 20, moved=10**5):
    single = not isinstance(outs, tuple)
    return pl.pallas_call(
        body,
        name=name,
        out_shape=outs,
        in_specs=in_specs,
        out_specs=IN_VMEM if single else (IN_VMEM,) * len(outs),
        scratch_shapes=list(scratch),
        compiler_params=pltpu.CompilerParams(vmem_limit_bytes=vmem),
        cost_estimate=pl.CostEstimate(flops=WORK[name] * 10**7, bytes_accessed=moved, transcendentals=0),
    )


def vmem(shape, dtype=F32):
    return pltpu.VMEM(shape, dtype)


def split(value):
    high = value.astype(BF16)
    low = (value - high.astype(F32)).astype(BF16)
    return high, low


def store_split(pair_ref, slot, value):
    rows = value.shape[0]
    high, low = split(value)
    pair_ref[slot, :rows] = high
    pair_ref[slot, rows:] = low


def product(pair_ref, slot, high_ref, low_ref, block, dims):
    rows = pair_ref.shape[1] // 2
    both = lax.dot_general(pair_ref[slot], high_ref[block], dims, preferred_element_type=F32)
    rest = lax.dot_general(
        pair_ref[slot, :rows], low_ref[block], dims, preferred_element_type=F32
    )
    return both[:rows] + both[rows:] + rest


def odd_device():
    return lax.rem(lax.axis_index("elem"), 2) == 1


def prepare_body(elem_total, nbr_ref, jac_ref, high_ref, low_ref, buffer, sems):
    elems = buffer.shape[0]
    copies = [
        [
            pltpu.make_async_copy(jac_ref.at[0, e, k], buffer.at[e, k], sems.at[e, k])
            for k in range(NBRS)
        ]
        for e in range(elems)
    ]
    for row in copies:
        for copy in row:
            copy.start()
    first = lax.axis_index("elem") * elems
    odd = odd_device()
    for e in range(elems):
        for k in range(NBRS):
            copies[e][k].wait()
            offset = lax.rem(nbr_ref[e, k] - (first + e) + RADIUS + elem_total, elem_total)
            slot = e * NBRS + offset
            slot = jnp.where(odd, elems * NBRS - 1 - slot, slot)
            high, low = split(buffer[e, k])
            high_ref[slot] = high
            low_ref[slot] = low


def mirror_body(field_ref, outer_ref, inner_ref):
    elems = field_ref.shape[0]
    odd = odd_device()
    for i in range(RADIUS):
        outer_ref[i] = field_ref[jnp.where(odd, elems - 1 - i, i)]
        inner_ref[i] = field_ref[jnp.where(odd, elems - 1 - RADIUS - i, RADIUS + i)]


def only(section, copies, body):
    def guarded(*refs):
        active = lax.axis_index("sec") == section

        @pl.when(active)
        def _():
            body(*refs)

        @pl.when(jnp.logical_not(active))
        def _():
            for source, target in copies:
                refs[target][...] = refs[source][...]

    return guarded


def block(e, m):
    return e * NBRS + m - e + RADIUS


def tangent_near_body(
    outer_ref, inner_ref, halo_ref, high_ref, low_ref, outer_out, inner_out, pair_ref
):
    elems = 2 * RADIUS
    for i in range(RADIUS):
        store_split(pair_ref, i, outer_ref[i])
        store_split(pair_ref, RADIUS + i, inner_ref[i])
        store_split(pair_ref, elems + RADIUS - 1 - i, halo_ref[i])
    for e in range(elems):
        total = outer_ref[e] if e < RADIUS else inner_ref[e - RADIUS]
        for m in range(max(0, e - RADIUS), e + RADIUS + 1):
            total += product(pair_ref, m, high_ref, low_ref, block(e, m), NT)
        if e < RADIUS:
            outer_out[e] = total
        else:
            inner_out[e - RADIUS] = total


def tangent_far_body(outer_ref, halo_ref, high_ref, low_ref, outer_out, pair_ref):
    for i in range(RADIUS):
        store_split(pair_ref, i, halo_ref[i])
    for e in range(RADIUS):
        total = outer_ref[e]
        for i in range(RADIUS - e):
            total += product(pair_ref, i, high_ref, low_ref, block(e, -1 - i), NT)
        outer_out[e] = total


def outer_products(pair_ref, high_ref, low_ref, out_ref):
    for i in range(RADIUS):
        total = None
        for e in range(RADIUS - i):
            term = product(pair_ref, e, high_ref, low_ref, block(e, -1 - i), NN)
            total = term if total is None else total + term
        out_ref[i] = total


def inner_products(pair_ref, high_ref, low_ref, out_ref, base):
    elems = 2 * RADIUS
    for i in range(RADIUS):
        m = elems + RADIUS - 1 - i
        total = None
        for e in range(m - RADIUS, elems):
            term = product(
                pair_ref, e - RADIUS + base, high_ref, low_ref, block(e, m), NN
            )
            total = term if total is None else total + term
        out_ref[i] = total


def observe_body(
    outer0_ref, inner0_ref, outer1_ref, inner1_ref, stations_ref, weights_ref, high_ref, low_ref,
    outer_out, inner_out, readings_ref, inner_send, pair_ref, state_ref,
):
    elems, cols, dofs = state_ref.shape
    count = weights_ref.shape[0]
    section = lax.axis_index("sec")

    @pl.when(section == 0)
    def _():
        state_ref[:RADIUS] = outer0_ref[...]
        state_ref[RADIUS:] = inner0_ref[...]

    @pl.when(section != 0)
    def _():
        state_ref[:RADIUS] = outer1_ref[...]
        state_ref[RADIUS:] = inner1_ref[...]

    flat = state_ref[...].reshape(elems * cols, dofs)
    weights = weights_ref[...]
    raw = lax.dot_general(flat, weights, NT, precision=PRECISE, preferred_element_type=F32)
    local = stations_ref[...] - lax.axis_index("elem") * elems
    odd = odd_device()
    readings = jnp.zeros((cols, count), F32)
    parts = []
    for u in range(elems):
        here = local == jnp.where(odd, elems - 1 - u, u)
        part = jnp.where(here, raw[u * cols : (u + 1) * cols], 0.0)
        readings += part
        parts.append(part)
    every = lax.dot_general(
        jnp.concatenate(parts, axis=0), weights, NN, precision=PRECISE, preferred_element_type=F32
    )
    for u in range(elems):
        seen = every[u * cols : (u + 1) * cols]
        if u < RADIUS:
            outer_out[u] = seen
        else:
            inner_out[u - RADIUS] = seen
            store_split(pair_ref, u - RADIUS, seen)
    readings_ref[...] = readings
    inner_products(pair_ref, high_ref, low_ref, inner_send, 0)


def seen_outer_body(value_ref, high_ref, low_ref, send_ref, pair_ref):
    for i in range(RADIUS):
        store_split(pair_ref, i, value_ref[i])
    outer_products(pair_ref, high_ref, low_ref, send_ref)


def adjoint_outer_body(total_ref, halo_ref, high_ref, low_ref, value_ref, send_ref, pair_ref):
    for i in range(RADIUS):
        value = total_ref[i] + halo_ref[i]
        value_ref[i] = value
        store_split(pair_ref, i, value)
    outer_products(pair_ref, high_ref, low_ref, send_ref)


def adjoint_inner_body(total_ref, halo_ref, high_ref, low_ref, value_ref, send_ref, pair_ref):
    for i in range(RADIUS):
        value = total_ref[i] + halo_ref[i]
        value_ref[i] = value
        store_split(pair_ref, i, value)
    inner_products(pair_ref, high_ref, low_ref, send_ref, 0)


def adjoint_local_body(outer_ref, inner_ref, high_ref, low_ref, outer_out, inner_out, pair_ref):
    elems = 2 * RADIUS
    for i in range(RADIUS):
        store_split(pair_ref, i, outer_ref[i])
        store_split(pair_ref, RADIUS + i, inner_ref[i])
    for m in range(elems):
        total = outer_ref[m] if m < RADIUS else inner_ref[m - RADIUS]
        for e in range(max(0, m - RADIUS), min(elems, m + RADIUS + 1)):
            total += product(pair_ref, e, high_ref, low_ref, block(e, m), NN)
        if m < RADIUS:
            outer_out[m] = total
        else:
            inner_out[m - RADIUS] = total


def finish_body(scale, field_ref, upper_ref, gram_ref, rest_ref, out_ref, gram_out):
    elems, cols, half = out_ref.shape
    odd = odd_device()
    first = lax.axis_index("sec") == 0
    for u in range(elems):
        place = jnp.where(odd, elems - 1 - u, u)
        out_ref[place] = jnp.where(first, field_ref[u, :, :half], upper_ref[u])
    gram_out[...] = (gram_ref[...] + rest_ref[...]) * scale


def gram_body(stack_ref, out_ref):
    own = lax.axis_index("col")
    places = []
    for j in range(stack_ref.shape[0]):
        away = jnp.bitwise_xor(own, j)
        places.append(
            jnp.bitwise_xor(away, jnp.bitwise_and(lax.shift_right_logical(away, 1), 2))
        )
    total = None
    for core in range(stack_ref.shape[1]):
        every = jnp.concatenate([stack_ref[place, core] for place in places], axis=0)
        term = lax.dot_general(
            stack_ref[0, core], every, NT, precision=PRECISE, preferred_element_type=F32
        )
        total = term if total is None else total + term
    out_ref[...] = total


def swap(value, axis, mask):
    count = lax.axis_size(axis)
    return lax.ppermute(value, axis, [(i, i ^ mask) for i in range(count)])


def off_chip(value):
    count = lax.axis_size("elem")
    pairs = [(i, (i + (1 if i % 2 else -1)) % count) for i in range(count)]
    return lax.ppermute(value, "elem", pairs)


def on_chip(value):
    return swap(value, "elem", 1)


def after(value, *others):
    return lax.optimization_barrier((value, *others))[0]


def per_device(probes, jacobian, neighbors, stations, obs_weights):
    cols, elems, dofs = probes.shape
    elem_total = elems * lax.axis_size("elem")
    blocks = elems * NBRS
    edge = vmem((RADIUS, cols, dofs))
    count = obs_weights.shape[0]
    half = dofs // 2
    col_count = lax.axis_size("col")

    def pair(slots):
        return pltpu.VMEM((slots, 2 * cols, dofs), BF16)

    prepare = call(
        functools.partial(prepare_body, elem_total), "prepare",
        (vmem((blocks, dofs, dofs), BF16),) * 2, [IN_SMEM, IN_HBM],
        (pltpu.VMEM((elems, NBRS, dofs, dofs), F32), pltpu.SemaphoreType.DMA((elems, NBRS))),
        vmem=46 << 20, moved=2 * 10**7,
    )
    mirror = call(mirror_body, "mirror", (edge, edge), [IN_VMEM])
    def make_tangent_near(body):
        return call(
            body, "tangent_near", (edge, edge), [IN_VMEM] * 5, (pair(9),),
        )

    tangent_near = make_tangent_near(only(1, ((0, 5), (1, 6)), tangent_near_body))
    tangent_near_first = make_tangent_near(only(0, ((0, 5), (1, 6)), tangent_near_body))
    def make_tangent_far(body):
        return call(
            body, "tangent_far", edge, [IN_VMEM] * 4, (pair(RADIUS),)
        )

    tangent_far = make_tangent_far(only(1, ((0, 4),), tangent_far_body))
    tangent_far_first = make_tangent_far(only(0, ((0, 4),), tangent_far_body))
    observe = call(
        observe_body, "observe", (edge, edge, vmem((cols, count)), edge), [IN_VMEM] * 8,
        (pair(RADIUS), pltpu.VMEM((elems, cols, dofs), F32)),
    )
    def make_adjoint_local(body):
        return call(
            body, "adjoint_local", (edge, edge), [IN_VMEM] * 4, (pair(elems),),
        )

    adjoint_local = make_adjoint_local(only(1, ((0, 4), (1, 5)), adjoint_local_body))
    adjoint_local_last = make_adjoint_local(only(0, ((0, 4), (1, 5)), adjoint_local_body))
    seen_products = call(
        seen_outer_body, "seen_outer", edge, [IN_VMEM] * 3, (pair(RADIUS),)
    )
    def make_adjoint_outer(body):
        return call(
            body, "adjoint_outer", (edge, edge), [IN_VMEM] * 4, (pair(RADIUS),),
        )

    adjoint_outer = make_adjoint_outer(only(1, ((0, 4), (1, 5)), adjoint_outer_body))
    adjoint_outer_last = make_adjoint_outer(only(0, ((0, 4), (1, 5)), adjoint_outer_body))
    def make_adjoint_inner(body):
        return call(
            body, "adjoint_inner", (edge, edge), [IN_VMEM] * 4, (pair(RADIUS),),
        )

    adjoint_inner = make_adjoint_inner(only(1, ((0, 4), (1, 5)), adjoint_inner_body))
    adjoint_inner_last = make_adjoint_inner(only(0, ((0, 4), (1, 5)), adjoint_inner_body))
    finish = call(
        functools.partial(finish_body, 1.0 / (elem_total * dofs)), "finish",
        (
            jax.ShapeDtypeStruct((elems, cols, half), F32),
            jax.ShapeDtypeStruct((cols, cols * col_count), F32),
        ),
        [IN_VMEM] * 4,
    )
    gram_part = call(gram_body, "gram_part", vmem((cols, cols * col_count)), [IN_VMEM])

    def tangent(outer, inner, high, low, near, far):
        for _ in range(STEPS):
            inner_in = on_chip(inner)
            outer_in = off_chip(outer)
            outer, inner = near(outer, inner, inner_in, high, low)
            outer = far(outer, outer_in, high, low)
        return outer, inner

    def to_next(outer, inner):
        inner = lax.ppermute(inner, "sec", [(0, 1)])
        return lax.ppermute(outer, "sec", [(0, 1)]), inner

    high, low = prepare(neighbors, jacobian)
    start = mirror(jnp.transpose(probes, (1, 0, 2)))
    state0 = tangent(*start, high, low, tangent_near_first, tangent_far_first)
    state1 = tangent(*to_next(*state0), high, low, tangent_near, tangent_far)
    seen_outer, seen_inner, readings, inner_send = observe(
        *state0, *state1, stations.reshape(1, count), obs_weights, high, low
    )

    def gather(stack, mask, *others):
        return jnp.concatenate([stack, swap(after(stack, *others), "col", mask)], axis=0)

    inner_in = on_chip(inner_send)
    stack = jnp.stack([readings, on_chip(readings)])[None]
    outer_in = off_chip(seen_products(seen_outer, high, low))
    outer, inner = adjoint_local(seen_outer, seen_inner, high, low)
    inner, inner_send = adjoint_inner(inner, inner_in, high, low)
    inner_in = on_chip(inner_send)
    stack = gather(stack, 1, inner_in)
    outer, outer_send = adjoint_outer(after(outer, inner_in), outer_in, high, low)
    outer_in = off_chip(outer_send)
    outer, inner = adjoint_local(outer, inner, high, low)
    inner = inner + inner_in
    inner_back = lax.ppermute(after(inner, outer_in), "sec", [(1, 0)])
    stack = gather(stack, 2, inner)
    outer = after(outer, inner) + outer_in
    outer_back = lax.ppermute(outer, "sec", [(1, 0)])
    stack = gather(stack, 6, outer)
    inner, inner_send = adjoint_inner_last(seen_inner, inner_back, high, low)
    inner_in = on_chip(inner_send)
    gram = gram_part(stack)
    gram = gram + swap(gram, "elem", 2)
    outer, outer_send = adjoint_outer_last(after(seen_outer, inner_send), outer_back, high, low)
    outer_in = off_chip(outer_send)
    outer, inner = adjoint_local_last(outer, inner, high, low)
    inner, inner_send = adjoint_inner_last(inner, inner_in, high, low)
    inner_in = on_chip(inner_send)
    gram = gram + swap(after(gram, inner_in), "elem", 4)
    outer, outer_send = adjoint_outer_last(after(outer, inner_in), outer_in, high, low)
    outer_in = off_chip(outer_send)
    outer, inner = adjoint_local_last(outer, inner, high, low)
    inner = inner + inner_in
    gram = gram + swap(after(gram, outer_in), "elem", 12)
    outer = after(outer, inner) + outer_in
    field = jnp.concatenate([outer, inner])
    upper = lax.ppermute(field[:, :, half:], "sec", [(0, 1)])
    hess, gram = finish(field, upper, gram, swap(gram, "sec", 1))
    return jnp.transpose(hess, (1, 0, 2)), gram


def solution(mesh):
    in_specs = (
        P("col", "elem", None),
        P("sec", "elem", None, None, None),
        P("elem", None),
        P("elem"),
        P("elem", None),
    )
    out_specs = (P("col", "elem", "sec"), P("col", None))
    return jax.shard_map(
        per_device, mesh=mesh, in_specs=in_specs, out_specs=out_specs, check_vma=False
    )
```
